32 devices in a mesh: lat: 8 (over y, x, core), lon: 4 (over z).
Axes of the slice: x: 2, y: 2, z: 4, core: 2. Of those that a mesh axis runs over, the one named last changes fastest.
Arguments:
- tracer: float32 [5, 16, 256, 2048], P(None, None, 'lat', 'lon'), may hold values from -6 to 6
- zonal_courant: float32 [16, 256, 2048], P(None, 'lat', 'lon'), may hold values from -1.5 to 1.5
- merid_courant: float32 [16, 256, 2048], P(None, 'lat', 'lon'), may hold values from -1.5 to 1.5
- filt_rows: int32 [64], replicated, may hold values from 0 to 255, as said below
- keep_modes: int32 [64], replicated, may hold values from 16 to 64, as said below
- reach: float32 [16], replicated, may hold values from 0.001 to 0.5, as said below
Outputs:
- updated: float32 [5, 16, 256, 2048], P(None, None, 'lat', 'lon')
The draws below stay inside these ranges and needn't reach their ends.
Inputs may be any that keep to these rules, and one draw needn't show every extreme that they name: filt_rows holds each of the 32 rows nearest each pole exactly once, in a drawn order. keep_modes[n] is the number of retained wavenumbers of row filt_rows[n]; both ends of the range are reached. reach is positive.
All inputs are finite; a program needn't handle non-finite values.
Results may differ from the reference program's by a relative error of at most 0.000057.
Values sent between devices are 32-bit elements; how exact they have to be, the bound alone decides.
No kernel may reach another device: no remote copies, remote signals or barrier semaphores. Data moves between devices by JAX's collectives and lax.ppermute only.
A program may use at most 128 MiB of HBM per device.

```python
import math
import jax
import jax.numpy as jnp
from jax import lax

NLON = 2048
FIELDS = 5
LEV = 16
KMAX = 64
LAT_DEV = 32
NLAT = 256


def filter_list(key):
    base_key = jax.random.fold_in(key, 7)
    shuffle = jax.random.permutation(jax.random.fold_in(base_key, 1), 2 * LAT_DEV)
    near_pole = jnp.arange(LAT_DEV, dtype=jnp.int32)
    polar_rows = jnp.concatenate([near_pole, NLAT - 1 - near_pole])
    row_list = polar_rows[shuffle]
    counts = jax.random.randint(jax.random.fold_in(base_key, 2), (2 * LAT_DEV,), KMAX // 4, KMAX + 1)
    chosen_slots = jax.random.permutation(jax.random.fold_in(base_key, 3), 2 * LAT_DEV)
    counts = counts.at[chosen_slots[0]].set(KMAX).at[chosen_slots[1]].set(KMAX // 4)
    return (row_list.astype(jnp.int32), counts.astype(jnp.int32))


def draw_filt_rows(key, part):
    return filter_list(key)[0]


def draw_keep_modes(key, part):
    return filter_list(key)[1]


def draw_reach(key, part):
    lowest, highest = (0.001, 0.5)
    uniform_draw = jax.random.uniform(key, (LEV,), jnp.float32)
    return jnp.exp(jnp.log(lowest) + uniform_draw * (jnp.log(highest) - jnp.log(lowest)))


def level_of(own_key, shape, split, smallest, top_value):
    factor_of, own = 1.0, jax.random.fold_in(own_key, 6)
    for axis_at, shards_of in split:
        draws = jnp.exp(jax.random.uniform(jax.random.fold_in(own, axis_at), (shards_of,), jnp.float32, smallest / len(split), top_value / len(split)))
        factor_of = factor_of * jnp.repeat(draws, shape[axis_at] // shards_of).reshape([-1 if axis == axis_at else 1 for axis in range(len(shape))])
    return factor_of


def scatter_about(stream_key, dims, spread, bound, pieces=(), kind=jnp.bfloat16):
    entries = spread * jax.random.normal(stream_key, dims, jnp.float32)
    if pieces:
        entries = entries * level_of(stream_key, dims, pieces, -0.22, 0.18)
    return jnp.clip(entries, -bound, bound).astype(kind)


def setup_inputs(seed: int = 0) -> dict:
    streams_of = jax.random.split(jax.random.key(seed), 7)
    return {
        "tracer": scatter_about(streams_of[0], (FIELDS, LEV, NLAT, NLON), 1.0, 6.0, ((2, 8), (3, 4)), jnp.float32),
        "zonal_courant": scatter_about(streams_of[1], (LEV, NLAT, NLON), 0.25, 1.5, ((1, 8), (2, 4)), jnp.float32),
        "merid_courant": scatter_about(streams_of[2], (LEV, NLAT, NLON), 0.25, 1.5, ((1, 8), (2, 4)), jnp.float32),
        "filt_rows": draw_filt_rows(jax.random.fold_in(streams_of[6], 71), 0),
        "keep_modes": draw_keep_modes(jax.random.fold_in(streams_of[6], 71), 0),
        "reach": draw_reach(jax.random.fold_in(streams_of[6], 71), 0),
    }


def reference(tracer, zonal_courant, merid_courant, filt_rows, keep_modes, reach):
    spacing = math.pi / NLAT
    row_float = jnp.arange(NLAT).astype(jnp.float32)
    centre_cos = jnp.sin((row_float + 0.5) * spacing)[:, None]
    north_face = jnp.sin((row_float + 1.0) * spacing)[:, None]
    south_face = jnp.sin(row_float * spacing)[:, None]
    matches = (jnp.arange(NLAT, dtype=jnp.int32)[:, None] == filt_rows[None, :]).astype(jnp.int32)
    retained = jnp.sum(matches * keep_modes[None, :], axis=1)
    wavenumber = jnp.arange(NLON // 2 + 1, dtype=jnp.int32)
    kept_modes = (wavenumber[None, :] < retained[:, None]) | (retained[:, None] == 0)
    coupling = (reach * NLON) ** 2
    wave_float = wavenumber.astype(jnp.float32)
    symbol = 1.0 + 4.0 * coupling[:, None] * jnp.sin(math.pi * wave_float / NLON)[None, :] ** 2

    def field_step(field_slab):
        zonal_flux = zonal_courant * field_slab
        merid_flux = merid_courant * field_slab
        zero_row = jnp.zeros_like(merid_flux[:, :1])
        above_flux = jnp.concatenate([merid_flux[:, 1:], zero_row], axis=1)
        below_flux = jnp.concatenate([zero_row, merid_flux[:, :-1]], axis=1)
        zonal_diff = jnp.roll(zonal_flux, -1, axis=2) - jnp.roll(zonal_flux, 1, axis=2)
        merid_diff = north_face * (merid_flux + above_flux) - south_face * (below_flux + merid_flux)
        tendency = -(zonal_diff + merid_diff) / (2.0 * centre_cos)
        spectrum = jnp.fft.rfft(tendency, axis=-1)
        spectrum = jnp.where(kept_modes[None], spectrum, 0.0) / symbol[:, None, :]
        return field_slab + jnp.fft.irfft(spectrum, n=NLON, axis=-1)

    return lax.map(field_step, tracer)
```

```python
import functools
import math

import jax
import jax.numpy as jnp
import numpy as np
from jax import lax
from jax.experimental import pallas as pl
from jax.experimental.pallas import tpu as pltpu
from jax.sharding import PartitionSpec as P

KMAX = 64
LANES = 128
AXES = ("lat", "lon")
f32 = jnp.float32
bf16 = jnp.bfloat16


def halves(array):
    hi = array.astype(bf16)
    return hi, (array - hi.astype(f32)).astype(bf16)


def wave_tables(cells, circle):
    angle = 2.0 * math.pi / circle * np.arange(KMAX)[None, :]
    at = np.arange(-1, cells + 1)[:, None] * angle
    waves = np.concatenate([np.cos(at), np.sin(at)], axis=1)
    forward = np.concatenate([waves[2:] - waves[:-2], waves[1:-1]], axis=0)
    return forward, waves[1:-1].T


def split_table(table):
    hi = table.astype(np.float32).astype(bf16)
    lo = (table - hi.astype(np.float64)).astype(np.float32).astype(bf16)
    return hi, lo


def metric_table(rows):
    row = np.arange(rows)
    table = np.zeros((rows, LANES))
    table[:, 0] = 0.5 / np.sin((row + 0.5) * math.pi / rows)
    table[:, 1] = np.sin((row + 1.0) * math.pi / rows)
    table[:, 2] = np.sin(row * math.pi / rows)
    return table.astype(np.float32)


def turn_table(parts, cells, circle):
    phase = 2.0 * math.pi / circle * ((np.arange(parts)[:, None] * cells * np.arange(KMAX)[None, :]) % circle)
    table = np.zeros((parts, 8, LANES))
    table[:, 0] = np.concatenate([np.cos(phase), np.cos(phase)], axis=1)
    table[:, 1] = np.concatenate([-np.sin(phase), np.sin(phase)], axis=1)
    return table.astype(np.float32)


def wave_numbers(circle):
    k = np.tile(np.arange(KMAX), 2)
    table = np.zeros((8, LANES))
    table[0] = 4.0 * np.sin(math.pi * k / circle) ** 2
    table[1] = np.where(k == 0, 1.0, 2.0) / circle
    return table.astype(np.float32)


def log_decay(reach, circle):
    u = 0.5 / (reach * circle)
    root = jnp.sqrt(1.0 + u * u)
    return -2.0 * jnp.log1p(u + u * u / (1.0 + root)), 4.0 * u * root


def lane_index(shape):
    return lax.broadcasted_iota(jnp.int32, shape, len(shape) - 1)


def row_index(shape):
    return lax.broadcasted_iota(jnp.int32, shape, len(shape) - 2)


def flux_rows(tracer, zonal, merid, below, above, north, south):
    rows = tracer.shape[0]
    at = row_index(tracer.shape)
    flux = merid * tracer
    up = jnp.where(at == rows - 1, above, pltpu.roll(flux, rows - 1, 0))
    face = north * (flux + up)
    first = south[0:1] * (below + flux[0:1])
    return zonal * tracer, jnp.where(at == 0, first, pltpu.roll(face, 1, 0)) - face


def project_kernel(circle, levels, has_sums, info, reach, tracer, zonal, merid, below, above, metric, turn, forward, *refs):
    if has_sums:
        prior, coeffs, sums, stack = refs
    else:
        coeffs, sums, stack = refs
    fields, per_step, rows, cells = tracer.shape
    signals = fields * rows
    step = pl.program_id(0)
    first_level = (info[1 + has_sums] * pl.num_programs(0) + step) * per_step
    north, south = metric[:, 1:2], metric[:, 2:3]

    def fluxes(i, f):
        level = pl.ds(first_level + i, 1)
        return flux_rows(tracer[f, i], zonal[i], merid[i], below[f, level], above[f, level], north, south)

    @pl.when(info[0] == 1)
    def _():
        for i in range(per_step):
            for f in range(fields):
                at = pl.ds((i * fields + f) * rows, rows)
                z, m = fluxes(i, f)
                stack[0, at, :cells], stack[1, at, :cells] = halves(z)
                stack[0, at, cells:], stack[1, at, cells:] = halves(m)
        table = forward[...]
        high = jnp.dot(stack[0], table, preferred_element_type=f32)
        low = jnp.dot(stack[1], table, preferred_element_type=f32)
        total = high[:, :LANES] + (high[:, LANES:] + low[:, :LANES] + low[:, LANES:])
        total = total * turn[0, 0:1] + pltpu.roll(total, KMAX, 1) * turn[0, 1:2]
        coeffs[...] = total.reshape(per_step, signals, LANES)

    @pl.when(info[0] == 0)
    def _():
        @pl.when(step == 0)
        def _():
            sums[...] = prior[...] if has_sums else jnp.zeros_like(sums)

        cell = lane_index((1, cells)).astype(f32)
        for i in range(per_step):
            level = first_level + i
            slope, gain = log_decay(jnp.full((1, cells), reach[level], f32), circle)
            eastward = jnp.exp((cells - 1.0 - cell) * slope)
            westward = jnp.exp(cell * slope)
            for f in range(fields):
                at = pl.ds(f * rows, rows)
                z, m = fluxes(i, f)
                z = z * gain
                right = jnp.sum((m + z) * eastward, axis=1, keepdims=True)
                left = jnp.sum((m - z) * westward, axis=1, keepdims=True)
                lane = lane_index((rows, LANES))
                sums[at, :] += jnp.where(lane == level, right, jnp.where(lane == level + KMAX, left, 0.0))


def finish_kernel(circle, levels, parts, second, info, reach, tracer, zonal, merid, below, above, metric, turn, backward, waves, rows_listed, kept, coeffs, sums, *refs):
    out, stack, enter = refs[-3:]
    fields, per_step, rows, cells = tracer.shape
    signals = fields * rows
    step = pl.program_id(0)
    first_level = (info[2 - second] * pl.num_programs(0) + step) * per_step
    scale, north, south = metric[:, 0:1], metric[:, 1:2], metric[:, 2:3]

    @pl.when(info[0] == 1)
    def _():
        row = info[3] + row_index((rows, 1))
        matches = row == rows_listed[...]
        retained = jnp.sum(jnp.where(matches, kept[...], 0), axis=1, keepdims=True)
        number = lane_index((rows, LANES)) % KMAX
        keep = jnp.where(number < retained, waves[1:2] * scale, 0.0)
        for i in range(per_step):
            coupling = (jnp.full((1, LANES), reach[first_level + i], f32) * circle) ** 2
            weight = keep / (1.0 + coupling * waves[0:1])
            for f in range(fields):
                at = pl.ds((i * fields + f) * rows, rows)
                c = coeffs[i, f * rows : (f + 1) * rows] * weight
                c = c * turn[0, 0:1] - pltpu.roll(c, KMAX, 1) * turn[0, 1:2]
                hi, lo = halves(c)
                stack[at, :LANES], stack[at, LANES : 2 * LANES] = hi, lo
                stack[at, 2 * LANES : 3 * LANES], stack[at, 3 * LANES : 4 * LANES] = hi, lo
        change = jnp.dot(stack[: per_step * signals, :], backward[...], preferred_element_type=f32)
        for i in range(per_step):
            for f in range(fields):
                at = (i * fields + f) * rows
                out[f, i] = tracer[f, i] + change[at : at + rows]

    @pl.when(info[0] == 0)
    def _():
        blocks = cells // LANES

        @pl.when(step == 0)
        def _():
            lane = lane_index((1, LANES))
            spread = jnp.ones((1, LANES), f32)
            for level in range(levels):
                spread = jnp.where(lane % KMAX == level, reach[level], spread)
            slope, _ = log_decay(spread, circle)
            wrap = 1.0 / (1.0 - jnp.exp(circle * slope))
            here = info[4]
            total = jnp.zeros((signals, LANES), f32)
            for p in range(parts):
                peer = here ^ p
                steps_up = lax.rem(here - peer - 1 + 2 * parts, parts).astype(f32)
                steps_down = lax.rem(peer - here - 1 + 2 * parts, parts).astype(f32)
                steps = jnp.where(lane < KMAX, steps_up, steps_down)
                total += sums[p] * (jnp.exp(steps * (cells * slope)) * wrap)
            enter[...] = total

        near = lane_index((LANES, LANES)) - row_index((LANES, LANES))
        lane = lane_index((1, LANES)).astype(f32)
        for i in range(per_step):
            level = first_level + i
            slope, gain = log_decay(jnp.full((1, LANES), reach[level], f32), circle)
            root = 1.0 / jnp.sqrt(1.0 + 4.0 * (jnp.full((1, LANES), reach[level], f32) * circle) ** 2)
            decay = jnp.exp(jnp.abs(near).astype(f32) * slope)
            turned = jnp.where(near > 0, gain, jnp.where(near < 0, -gain, 0.0)) * decay
            zhi, zlo = halves(turned)
            mhi, mlo = halves(decay)
            table = jnp.concatenate([jnp.concatenate([zhi, zlo], axis=1), jnp.concatenate([mhi, mlo], axis=1)], axis=0)
            for f in range(fields):
                level_at = pl.ds(level, 1)
                z, m = flux_rows(tracer[f, i], zonal[i], merid[i], below[f, level_at], above[f, level_at], north, south)
                for b in range(blocks):
                    at = (b * fields + f) * rows
                    own = slice(b * LANES, (b + 1) * LANES)
                    hi, lo = halves(z[:, own])
                    stack[at : at + rows, :LANES], stack[at : at + rows, 2 * LANES : 3 * LANES] = hi, lo
                    hi, lo = halves(m[:, own])
                    stack[at : at + rows, LANES : 2 * LANES], stack[at : at + rows, 3 * LANES : 4 * LANES] = hi, lo
            used = blocks * signals
            high = jnp.dot(stack[:used, : 2 * LANES], table, preferred_element_type=f32)
            low = jnp.dot(stack[:used, 2 * LANES :], table, preferred_element_type=f32)
            local = high[:, :LANES] + (high[:, LANES:] + low[:, :LANES] + low[:, LANES:])
            from_west = jnp.exp((lane + 1.0) * slope)
            from_east = jnp.exp((LANES - lane) * slope)
            across = jnp.exp(LANES * slope)[:, 0:1]
            size = root * scale
            edge = gain[:, 0:1]
            pick = lane_index((rows, LANES))
            for f in range(fields):
                entering = enter[f * rows : (f + 1) * rows]
                part = [local[(b * fields + f) * rows : (b * fields + f + 1) * rows] for b in range(blocks)]
                carry = jnp.sum(jnp.where(pick == level, entering, 0.0), axis=1, keepdims=True)
                ups = []
                for b in range(blocks):
                    ups.append(carry)
                    last = slice((b + 1) * LANES - 1, (b + 1) * LANES)
                    flux = zonal[i, :, last] * tracer[f, i, :, last]
                    carry = across * carry + (part[b][:, LANES - 1 :] + edge * flux)
                carry = jnp.sum(jnp.where(pick == level + KMAX, entering, 0.0), axis=1, keepdims=True)
                for b in reversed(range(blocks)):
                    own = slice(b * LANES, (b + 1) * LANES)
                    change = part[b] + from_west * ups[b] + from_east * carry
                    out[f, i, :, own] = tracer[f, i, :, own] + size * change
                    first = slice(b * LANES, b * LANES + 1)
                    flux = zonal[i, :, first] * tracer[f, i, :, first]
                    carry = across * carry + (part[b][:, :1] - edge * flux)


def swapped(array, bit, lats, parts):
    pairs = [(lat * parts + p, lat * parts + (p ^ bit)) for lat in lats for p in range(parts)]
    return lax.ppermute(array, AXES, pairs)


def on_device(tracer, zonal, merid, filt_rows, keep_modes, reach):
    fields, levels, rows, cells = tracer.shape
    bands, parts = lax.axis_size("lat"), lax.axis_size("lon")
    circle, signals = cells * parts, fields * rows
    listed = filt_rows.shape[0]
    assert listed == 2 * rows and levels <= KMAX and cells % LANES == 0
    assert parts >= 2 and parts & (parts - 1) == 0 and bands > 2
    band, place = lax.axis_index("lat"), lax.axis_index("lon")
    polar = jnp.logical_or(band == 0, band == bands - 1).astype(jnp.int32)
    bit = (place & 1) * polar
    info = jnp.stack([polar, 1 - bit, bit, band * rows, place, band]).astype(jnp.int32)
    poles, inner = (0, bands - 1), range(1, bands - 1)

    first = merid[None, :, 0] * tracer[:, :, 0]
    last = merid[None, :, -1] * tracer[:, :, -1]
    below = lax.ppermute(last, "lat", [(i, i + 1) for i in range(bands - 1)])
    above = lax.ppermute(first, "lat", [(i + 1, i) for i in range(bands - 1)])

    forward, waves_at = wave_tables(cells, circle)
    forward = jnp.asarray(np.concatenate(split_table(forward), axis=1))
    hi, lo = split_table(waves_at)
    backward = jnp.asarray(np.concatenate([hi, hi, lo, lo], axis=0))
    metric = jnp.asarray(metric_table(rows * bands))
    turn = jnp.asarray(turn_table(parts, cells, circle))
    waves = jnp.asarray(wave_numbers(circle))

    per_step = 2
    steps = levels // 2 // per_step
    assert levels % (2 * per_step) == 0
    whole = lambda shape: pl.BlockSpec(shape, lambda s, *_: (0,) * len(shape))

    def common(half):
        at = lambda s, info, *_: info[half] * steps + s
        return [
            pl.BlockSpec((fields, per_step, rows, cells), lambda s, *a: (0, at(s, *a), 0, 0)),
            pl.BlockSpec((per_step, rows, cells), lambda s, *a: (at(s, *a), 0, 0)),
            pl.BlockSpec((per_step, rows, cells), lambda s, *a: (at(s, *a), 0, 0)),
            whole((fields, levels, cells)),
            whole((fields, levels, cells)),
            pl.BlockSpec((rows, LANES), lambda s, info, *_: (info[5], 0)),
            pl.BlockSpec((1, 8, LANES), lambda s, info, *_: (info[4], 0, 0)),
        ]

    def project(second, *prior):
        sums = jax.ShapeDtypeStruct((signals, LANES), f32)
        return pl.pallas_call(
            functools.partial(project_kernel, circle, levels, second),
            out_shape=(jax.ShapeDtypeStruct((levels // 2, signals, LANES), f32), sums),
            grid_spec=pltpu.PrefetchScalarGridSpec(
                num_scalar_prefetch=2,
                grid=(steps,),
                in_specs=common(1 + second) + [whole((2 * cells, 2 * LANES))] + [whole((signals, LANES)) for _ in prior],
                out_specs=(
                    pl.BlockSpec((per_step, signals, LANES), lambda s, *_: (s, 0, 0)),
                    whole((signals, LANES)),
                ),
                scratch_shapes=[pltpu.VMEM((2, per_step * signals, 2 * cells), bf16)],
            ),
            compiler_params=pltpu.CompilerParams(vmem_limit_bytes=40 << 20),
            name="project_rest" if second else "project_sent",
        )(info, reach, tracer, zonal, merid, below, above, metric, turn, forward, *prior)

    sent, sums = project(0)
    received = swapped(sent, 1, poles, parts)
    own, sums = project(1, sums)

    gathered = sums[None]
    step = 1
    while step < parts:
        gathered = jnp.concatenate([gathered, swapped(gathered, step, inner, parts)], axis=0)
        step *= 2

    total = own + received
    step, stacked = 2, []
    while 2 * step < parts:
        half = total.shape[0] // 2
        side = (place // step) & 1
        mine = lax.dynamic_slice_in_dim(total, side * half, half, 0)
        other = lax.dynamic_slice_in_dim(total, (1 - side) * half, half, 0)
        total = mine + swapped(other, step, poles, parts)
        stacked.append(step)
        step *= 2
    if step < parts:
        total = total + swapped(total, step, poles, parts)
    for step in reversed(stacked):
        back = swapped(total, step, poles, parts)
        side = ((place // step) & 1) == 0
        total = jnp.concatenate([jnp.where(side, total, back), jnp.where(side, back, total)], axis=0)
    rest = swapped(total, 1, poles, parts)

    def finish(second, coeffs, *prior):
        at = lambda s, info, *_: info[2 - second] * steps + s
        return pl.pallas_call(
            functools.partial(finish_kernel, circle, levels, parts, second),
            out_shape=jax.ShapeDtypeStruct(tracer.shape, f32),
            grid_spec=pltpu.PrefetchScalarGridSpec(
                num_scalar_prefetch=2,
                grid=(steps,),
                in_specs=common(2 - second)
                + [
                    whole((4 * LANES, cells)),
                    whole((8, LANES)),
                    whole((1, listed)),
                    whole((1, listed)),
                    pl.BlockSpec((per_step, signals, LANES), lambda s, *_: (s, 0, 0)),
                    whole((parts, signals, LANES)),
                ]
                + [pl.BlockSpec(memory_space=pl.ANY) for _ in prior],
                out_specs=pl.BlockSpec((fields, per_step, rows, cells), lambda s, *a: (0, at(s, *a), 0, 0)),
                scratch_shapes=[
                    pltpu.VMEM((max(cells // LANES, per_step) * signals, 4 * LANES), bf16),
                    pltpu.VMEM((signals, LANES), f32),
                ],
            ),
            input_output_aliases={15: 0} if prior else {},
            compiler_params=pltpu.CompilerParams(vmem_limit_bytes=40 << 20),
            name="finish_rest" if second else "finish_own",
        )(
            info, reach, tracer, zonal, merid, below, above, metric, turn, backward, waves,
            filt_rows.reshape(1, listed), keep_modes.reshape(1, listed), coeffs, gathered, *prior,
        )

    return finish(1, rest, finish(0, total))


def solution(mesh):
    return jax.shard_map(
        on_device,
        mesh=mesh,
        in_specs=(
            P(None, None, "lat", "lon"),
            P(None, "lat", "lon"),
            P(None, "lat", "lon"),
            P(),
            P(),
            P(),
        ),
        out_specs=P(None, None, "lat", "lon"),
        check_vma=False,
    )
```

```python
import functools
import math

import jax
import jax.numpy as jnp
import numpy as np
from jax import lax
from jax.experimental import pallas as pl
from jax.experimental.pallas import tpu as pltpu
from jax.sharding import PartitionSpec as P

KMAX = 64
LANES = 128
PER_STEP = 2
VMEM_LIMIT = 24 << 20
AXES = ("lat", "lon")
f32 = jnp.float32
bf16 = jnp.bfloat16


def halves(array):
    hi = array.astype(bf16)
    return hi, (array - hi.astype(f32)).astype(bf16)


def wave_tables(cells, circle):
    angle = 2.0 * math.pi / circle * np.arange(KMAX)[None, :]
    at = np.arange(-1, cells + 1)[:, None] * angle
    waves = np.concatenate([np.cos(at), np.sin(at)], axis=1)
    forward = np.concatenate([waves[2:] - waves[:-2], waves[1:-1]], axis=0)
    return forward, waves[1:-1].T


def split_table(table):
    hi = table.astype(np.float32).astype(bf16)
    lo = (table - hi.astype(np.float64)).astype(np.float32).astype(bf16)
    return hi, lo


def metric_table(rows):
    row = np.arange(rows)
    table = np.zeros((rows, LANES))
    table[:, 0] = 0.5 / np.sin((row + 0.5) * math.pi / rows)
    table[:, 1] = np.sin((row + 1.0) * math.pi / rows)
    table[:, 2] = np.sin(row * math.pi / rows)
    return table.astype(np.float32)


def turn_table(parts, cells, circle):
    phase = 2.0 * math.pi / circle * ((np.arange(parts)[:, None] * cells * np.arange(KMAX)[None, :]) % circle)
    table = np.zeros((parts, 8, LANES))
    table[:, 0] = np.concatenate([np.cos(phase), np.cos(phase)], axis=1)
    table[:, 1] = np.concatenate([-np.sin(phase), np.sin(phase)], axis=1)
    return table.astype(np.float32)


def wave_numbers(circle):
    k = np.tile(np.arange(KMAX), 2)
    table = np.zeros((8, LANES))
    table[0] = 4.0 * np.sin(math.pi * k / circle) ** 2
    table[1] = np.where(k == 0, 1.0, 2.0) / circle
    return table.astype(np.float32)


def log_decay(reach, circle):
    u = 0.5 / (reach * circle)
    root = jnp.sqrt(1.0 + u * u)
    return -2.0 * jnp.log1p(u + u * u / (1.0 + root)), 4.0 * u * root


def lane_index(shape):
    return lax.broadcasted_iota(jnp.int32, shape, len(shape) - 1)


def row_index(shape):
    return lax.broadcasted_iota(jnp.int32, shape, len(shape) - 2)


def flux_rows(tracer, zonal, merid, below, above, north, south):
    rows = tracer.shape[0]
    at = row_index(tracer.shape)
    flux = merid * tracer
    up = jnp.where(at == rows - 1, above, pltpu.roll(flux, rows - 1, 0))
    face = north * (flux + up)
    first = south[0:1] * (below + flux[0:1])
    return zonal * tracer, jnp.where(at == 0, first, pltpu.roll(face, 1, 0)) - face


def edge_kernel(tracer, merid, first, last, tracer_rows, merid_rows, sems):
    fields, _, rows, _ = tracer.shape
    tall = tracer_rows.shape[3]
    copies = []
    for side, at in enumerate((0, rows - tall)):
        copies.append(pltpu.make_async_copy(merid.at[:, pl.ds(at, tall)], merid_rows.at[side], sems.at[side]))
        copies.append(
            pltpu.make_async_copy(tracer.at[:, :, pl.ds(at, tall)], tracer_rows.at[side], sems.at[2 + side])
        )
    for copy in copies:
        copy.start()
    for side, (out, at) in enumerate(((first, 0), (last, tall - 1))):
        copies[2 * side].wait()
        copies[2 * side + 1].wait()
        for f in range(fields):
            out[f] = merid_rows[side, :, at] * tracer_rows[side, f, :, at]


def fetch_kernel(count, *refs):
    sems = refs[-1]
    copies = [pltpu.make_async_copy(refs[i], refs[count + i], sems.at[i]) for i in range(count)]
    for copy in copies:
        copy.start()
    for copy in copies:
        copy.wait()


def project_kernel(circle, base, last, info, reach, tracer, zonal, merid, below, above, metric, turn, forward, *refs):
    if last:
        prior, coeffs, sums, stack, total_sums = refs
    else:
        coeffs, total_sums, stack = refs
    fields, levels, rows, cells = tracer.shape
    signals = fields * rows
    size = coeffs.shape[0]
    first_level = info[base]
    rows_at = pl.ds(info[2], rows)

    def fluxes(level, f):
        north, south = metric[rows_at, 1:2], metric[rows_at, 2:3]
        at = pl.ds(level, 1)
        return flux_rows(tracer[f, level], zonal[level], merid[level], below[f, at], above[f, at], north, south)

    @pl.when(info[0] == 1)
    def _():
        table = forward[...]
        turn_cos, turn_sin = turn[info[1], 0:1], turn[info[1], 1:2]
        for group in range(size // PER_STEP):
            slot = 2 * (group % 2)
            for i in range(PER_STEP):
                for f in range(fields):
                    at = pl.ds((i * fields + f) * rows, rows)
                    z, m = fluxes(first_level + group * PER_STEP + i, f)
                    stack[slot, at, :cells], stack[slot + 1, at, :cells] = halves(z)
                    stack[slot, at, cells:], stack[slot + 1, at, cells:] = halves(m)
            high = jnp.dot(stack[slot], table, preferred_element_type=f32)
            low = jnp.dot(stack[slot + 1], table, preferred_element_type=f32)
            total = high[:, :LANES] + (high[:, LANES:] + low[:, :LANES] + low[:, LANES:])
            total = total * turn_cos + pltpu.roll(total, KMAX, 1) * turn_sin
            coeffs[group * PER_STEP : (group + 1) * PER_STEP] = total.reshape(PER_STEP, signals, LANES)

    @pl.when(info[0] == 0)
    def _():
        total_sums[...] = prior[...] if last else jnp.zeros_like(total_sums)
        cell = lane_index((1, cells)).astype(f32)
        lane = lane_index((rows, LANES))

        def one(i, _):
            level = first_level + i
            slope, gain = log_decay(jnp.full((1, cells), reach[level], f32), circle)
            eastward = jnp.exp((cells - 1.0 - cell) * slope)
            westward = jnp.exp(cell * slope)
            for f in range(fields):
                at = pl.ds(f * rows, rows)
                z, m = fluxes(level, f)
                z = z * gain
                right = jnp.sum((m + z) * eastward, axis=1, keepdims=True)
                left = jnp.sum((m - z) * westward, axis=1, keepdims=True)
                total_sums[at, :] += jnp.where(lane == level, right, jnp.where(lane == level + levels, left, 0.0))
            return 0

        lax.fori_loop(0, size, one, 0)
        if last:
            sums[...] = jnp.transpose(total_sums[...])[: 2 * levels]


def finish_kernel(circle, parts, base, size, info, reach, tracer, zonal, merid, below, above, metric, turn, backward, waves, rows_listed, kept, coeffs, sums, *refs):
    out, stack, enter, ready, sems = refs[-5:]
    fields, levels, rows, cells = tracer.shape
    signals = fields * rows
    first_level = info[base]
    rows_at = pl.ds(info[2], rows)

    def send(i, count):
        return pltpu.make_async_copy(
            ready.at[:, pl.ds(i, count)], out.at[:, pl.ds(first_level + i, count)], sems.at[i]
        )

    @pl.when(info[0] == 1)
    def _():
        scale = metric[rows_at, 0:1]
        turn_cos, turn_sin = turn[info[1], 0:1], turn[info[1], 1:2]
        row = info[2] + row_index((rows, 1))
        matches = row == rows_listed[...]
        retained = jnp.sum(jnp.where(matches, kept[...], 0), axis=1, keepdims=True)
        number = lane_index((rows, LANES)) % KMAX
        keep = jnp.where(number < retained, waves[1:2] * scale, 0.0)
        for group in range(size // PER_STEP):
            slot = group % 2
            for i in range(PER_STEP):
                level = first_level + group * PER_STEP + i
                coupling = (jnp.full((1, LANES), reach[level], f32) * circle) ** 2
                weight = keep / (1.0 + coupling * waves[0:1])
                for f in range(fields):
                    at = pl.ds((i * fields + f) * rows, rows)
                    c = coeffs[group * PER_STEP + i, f * rows : (f + 1) * rows] * weight
                    c = c * turn_cos - pltpu.roll(c, KMAX, 1) * turn_sin
                    hi, lo = halves(c)
                    stack[slot, at, :LANES], stack[slot, at, LANES : 2 * LANES] = hi, lo
                    stack[slot, at, 2 * LANES : 3 * LANES], stack[slot, at, 3 * LANES :] = hi, lo
            change = jnp.dot(stack[slot, : PER_STEP * signals], backward[...], preferred_element_type=f32)
            for i in range(PER_STEP):
                for f in range(fields):
                    at = (i * fields + f) * rows
                    level = group * PER_STEP + i
                    ready[f, level] = tracer[f, first_level + level] + change[at : at + rows]
            send(group * PER_STEP, PER_STEP).start()
        for group in range(size // PER_STEP):
            send(group * PER_STEP, PER_STEP).wait()

    @pl.when(info[0] == 0)
    def _():
        scale, north, south = metric[rows_at, 0:1], metric[rows_at, 1:2], metric[rows_at, 2:3]
        blocks = cells // LANES
        wide = sums.shape[2] // LANES
        listed = row_index((2 * levels, LANES))
        spread = jnp.ones((2 * levels, LANES), f32)
        for level in range(levels):
            spread = jnp.where(listed % levels == level, reach[level], spread)
        slopes, _ = log_decay(spread, circle)
        wrap = 1.0 / (1.0 - jnp.exp(circle * slopes))
        here = info[1]
        total = jnp.zeros(sums.shape[1:], f32)
        for p in range(parts):
            peer = here ^ p
            steps_up = lax.rem(here - peer - 1 + 2 * parts, parts).astype(f32)
            steps_down = lax.rem(peer - here - 1 + 2 * parts, parts).astype(f32)
            steps = jnp.where(listed < levels, steps_up, steps_down)
            weight = jnp.exp(steps * (cells * slopes)) * wrap
            total += sums[p] * jnp.concatenate([weight] * wide, axis=1)
        pad = jnp.zeros((LANES - 2 * levels, wide * LANES), f32)
        enter[...] = jnp.transpose(jnp.concatenate([total, pad], axis=0))

        near = lane_index((LANES, LANES)) - row_index((LANES, LANES))
        lane = lane_index((1, LANES)).astype(f32)
        pick = lane_index((rows, LANES))

        def one(i, _):
            level = first_level + i
            level_at = pl.ds(level, 1)
            slope, gain = log_decay(jnp.full((1, LANES), reach[level], f32), circle)
            root = 1.0 / jnp.sqrt(1.0 + 4.0 * (jnp.full((1, LANES), reach[level], f32) * circle) ** 2)
            decay = jnp.exp(jnp.abs(near).astype(f32) * slope)
            turned = jnp.where(near > 0, gain, jnp.where(near < 0, -gain, 0.0)) * decay
            zhi, zlo = halves(turned)
            mhi, mlo = halves(decay)
            table = jnp.concatenate([jnp.concatenate([zhi, zlo], axis=1), jnp.concatenate([mhi, mlo], axis=1)], axis=0)
            for f in range(fields):
                z, m = flux_rows(
                    tracer[f, level], zonal[level], merid[level], below[f, level_at], above[f, level_at], north, south
                )
                for b in range(blocks):
                    at = slice((b * fields + f) * rows, (b * fields + f + 1) * rows)
                    own = slice(b * LANES, (b + 1) * LANES)
                    hi, lo = halves(z[:, own])
                    stack[0, at, :LANES], stack[0, at, 2 * LANES : 3 * LANES] = hi, lo
                    hi, lo = halves(m[:, own])
                    stack[0, at, LANES : 2 * LANES], stack[0, at, 3 * LANES :] = hi, lo
            used = blocks * signals
            high = jnp.dot(stack[0, :used, : 2 * LANES], table, preferred_element_type=f32)
            low = jnp.dot(stack[0, :used, 2 * LANES :], table, preferred_element_type=f32)
            local = high[:, :LANES] + (high[:, LANES:] + low[:, :LANES] + low[:, LANES:])
            from_west = jnp.exp((lane + 1.0) * slope)
            from_east = jnp.exp((LANES - lane) * slope)
            across = jnp.exp(LANES * slope)[:, 0:1]
            size_of = root * scale
            edge = gain[:, 0:1]
            for f in range(fields):
                entering = enter[f * rows : (f + 1) * rows]
                part = [local[(b * fields + f) * rows : (b * fields + f + 1) * rows] for b in range(blocks)]
                carry = jnp.sum(jnp.where(pick == level, entering, 0.0), axis=1, keepdims=True)
                ups = []
                for b in range(blocks):
                    ups.append(carry)
                    cell = slice((b + 1) * LANES - 1, (b + 1) * LANES)
                    flux = zonal[level, :, cell] * tracer[f, level, :, cell]
                    carry = across * carry + (part[b][:, LANES - 1 :] + edge * flux)
                carry = jnp.sum(jnp.where(pick == level + levels, entering, 0.0), axis=1, keepdims=True)
                for b in reversed(range(blocks)):
                    own = slice(b * LANES, (b + 1) * LANES)
                    change = part[b] + from_west * ups[b] + from_east * carry
                    ready[f, i, :, own] = tracer[f, level, :, own] + size_of * change
                    cell = slice(b * LANES, b * LANES + 1)
                    flux = zonal[level, :, cell] * tracer[f, level, :, cell]
                    carry = across * carry + (part[b][:, :1] - edge * flux)
            send(i, 1).start()
            return 0

        lax.fori_loop(0, size, one, 0)
        for i in range(size):
            send(i, 1).wait()


def swapped(array, bit, lats, parts):
    pairs = [(lat * parts + p, lat * parts + (p ^ bit)) for lat in lats for p in range(parts)]
    return lax.ppermute(array, AXES, pairs)


def on_device(tracer, zonal, merid, filt_rows, keep_modes, reach):
    fields, levels, rows, cells = tracer.shape
    bands, parts = lax.axis_size("lat"), lax.axis_size("lon")
    circle, signals = cells * parts, fields * rows
    padded = -(-signals // LANES) * LANES
    listed = filt_rows.shape[0]
    assert listed == 2 * rows and 2 * levels <= LANES and cells % LANES == 0
    assert parts >= 2 and parts & (parts - 1) == 0 and bands > 2 and rows % 8 == 0
    band, place = lax.axis_index("lat"), lax.axis_index("lon")
    polar = jnp.logical_or(band == 0, band == bands - 1).astype(jnp.int32)
    bit = (place & 1) * polar
    half = levels // 2
    assert levels % (2 * PER_STEP) == 0
    info = jnp.stack([polar, place, band * rows, (1 - bit) * half, bit * half]).astype(jnp.int32)
    sent_at, own_at = 3, 4
    poles, inner = (0, bands - 1), range(1, bands - 1)

    smem, vmem, hbm = (pl.BlockSpec(memory_space=space) for space in (pltpu.SMEM, pltpu.VMEM, pltpu.HBM))
    params = pltpu.CompilerParams(vmem_limit_bytes=VMEM_LIMIT)
    dma = pltpu.SemaphoreType.DMA

    tall = 8
    resident = lambda array: pltpu.with_memory_space_constraint(array, pltpu.HBM)
    first, last = pl.pallas_call(
        edge_kernel,
        out_shape=(jax.ShapeDtypeStruct((fields, levels, cells), f32),) * 2,
        in_specs=[hbm, hbm],
        out_specs=(vmem, vmem),
        scratch_shapes=[
            pltpu.VMEM((2, fields, levels, tall, cells), f32),
            pltpu.VMEM((2, levels, tall, cells), f32),
            dma((4,)),
        ],
        compiler_params=params,
        name="edges",
    )(resident(tracer), resident(merid))
    below = lax.ppermute(last, "lat", [(i, i + 1) for i in range(bands - 1)])
    above = lax.ppermute(first, "lat", [(i + 1, i) for i in range(bands - 1)])
    forward, waves_at = wave_tables(cells, circle)
    forward = jnp.asarray(np.concatenate(split_table(forward), axis=1))
    hi, lo = split_table(waves_at)
    backward = jnp.asarray(np.concatenate([hi, hi, lo, lo], axis=0))
    metric = jnp.asarray(metric_table(rows * bands))
    turn = jnp.asarray(turn_table(parts, cells, circle))
    waves = jnp.asarray(wave_numbers(circle))
    arrays = (tracer, zonal, merid, forward, backward, metric, turn, waves)
    tracer, zonal, merid, forward, backward, metric, turn, waves = pl.pallas_call(
        functools.partial(fetch_kernel, len(arrays)),
        out_shape=tuple(pltpu.VMEM(array.shape, array.dtype) for array in arrays),
        in_specs=[hbm] * len(arrays),
        out_specs=(vmem,) * len(arrays),
        scratch_shapes=[dma((len(arrays),))],
        compiler_params=params,
        cost_estimate=pl.CostEstimate(flops=0, transcendentals=0, bytes_accessed=16 << 20),
        name="fetch",
    )(*map(resident, arrays))

    def project(base, *prior):
        if prior:
            sums = jax.ShapeDtypeStruct((2 * levels, padded), f32)
            extra = [pltpu.VMEM((padded, LANES), f32)]
        else:
            sums = jax.ShapeDtypeStruct((padded, LANES), f32)
            extra = []
        return pl.pallas_call(
            functools.partial(project_kernel, circle, base, bool(prior)),
            out_shape=(jax.ShapeDtypeStruct((half, signals, LANES), f32), sums),
            in_specs=[smem] * 2 + [vmem] * (8 + len(prior)),
            out_specs=(vmem, vmem),
            scratch_shapes=[pltpu.VMEM((4, PER_STEP * signals, 2 * cells), bf16)] + extra,
            compiler_params=params,
            name="project",
        )(info, reach, tracer, zonal, merid, below, above, metric, turn, forward, *prior)

    def finish(base, coeffs, *prior):
        return pl.pallas_call(
            functools.partial(finish_kernel, circle, parts, base, half),
            out_shape=jax.ShapeDtypeStruct(tracer.shape, f32),
            in_specs=[smem] * 2 + [vmem] * 13 + [hbm] * len(prior),
            out_specs=hbm,
            scratch_shapes=[
                pltpu.VMEM((2, max(cells // LANES, PER_STEP) * signals, 4 * LANES), bf16),
                pltpu.VMEM((padded, LANES), f32),
                pltpu.VMEM((fields, half, rows, cells), f32),
                dma((half,)),
            ],
            input_output_aliases={15: 0} if prior else {},
            compiler_params=params,
            name="finish",
        )(
            info, reach, tracer, zonal, merid, below, above, metric, turn, backward, waves,
            filt_rows.reshape(1, listed), keep_modes.reshape(1, listed), coeffs, gathered, *prior,
        )

    sent, sums = project(sent_at)
    received = swapped(sent, 1, poles, parts)
    own, sums = project(own_at, sums)

    gathered = sums[None]
    step = 1
    while step < parts:
        gathered = jnp.concatenate([gathered, swapped(gathered, step, inner, parts)], axis=0)
        step *= 2

    total = own + received
    step, stacked = 2, []
    while 2 * step < parts:
        size = total.shape[0] // 2
        side = (place // step) & 1
        mine = lax.dynamic_slice_in_dim(total, side * size, size, 0)
        other = lax.dynamic_slice_in_dim(total, (1 - side) * size, size, 0)
        total = mine + swapped(other, step, poles, parts)
        stacked.append(step)
        step *= 2
    if step < parts:
        total = total + swapped(total, step, poles, parts)
    for step in reversed(stacked):
        back = swapped(total, step, poles, parts)
        side = ((place // step) & 1) == 0
        total = jnp.concatenate([jnp.where(side, total, back), jnp.where(side, back, total)], axis=0)
    rest = swapped(total, 1, poles, parts)
    return finish(sent_at, rest, finish(own_at, total))


def solution(mesh):
    return jax.shard_map(
        on_device,
        mesh=mesh,
        in_specs=(
            P(None, None, "lat", "lon"),
            P(None, "lat", "lon"),
            P(None, "lat", "lon"),
            P(),
            P(),
            P(),
        ),
        out_specs=P(None, None, "lat", "lon"),
        check_vma=False,
    )
```

```python
import functools
import math

import jax
import jax.numpy as jnp
import numpy as np
from jax import lax
from jax.experimental import pallas as pl
from jax.experimental.pallas import tpu as pltpu
from jax.sharding import PartitionSpec as P

KMAX = 64
LANES = 128
PER_STEP = 2
CHUNKS = 2
VMEM_LIMIT = 16 << 20
AXES = ("lat", "lon")
f32 = jnp.float32
bf16 = jnp.bfloat16


def halves(array):
    hi = array.astype(bf16)
    return hi, (array - hi.astype(f32)).astype(bf16)


def wave_tables(cells, circle):
    angle = 2.0 * math.pi / circle * np.arange(KMAX)[None, :]
    at = np.arange(-1, cells + 1)[:, None] * angle
    waves = np.concatenate([np.cos(at), np.sin(at)], axis=1)
    forward = np.concatenate([waves[2:] - waves[:-2], waves[1:-1]], axis=0)
    return forward, waves[1:-1].T


def split_table(table):
    hi = table.astype(np.float32).astype(bf16)
    lo = (table - hi.astype(np.float64)).astype(np.float32).astype(bf16)
    return hi, lo


def metric_table(rows):
    row = np.arange(rows)
    table = np.zeros((rows, LANES))
    table[:, 0] = 0.5 / np.sin((row + 0.5) * math.pi / rows)
    table[:, 1] = np.sin((row + 1.0) * math.pi / rows)
    table[:, 2] = np.sin(row * math.pi / rows)
    return table.astype(np.float32)


def turn_table(parts, cells, circle):
    phase = 2.0 * math.pi / circle * ((np.arange(parts)[:, None] * cells * np.arange(KMAX)[None, :]) % circle)
    table = np.zeros((parts, 8, LANES))
    table[:, 0] = np.concatenate([np.cos(phase), np.cos(phase)], axis=1)
    table[:, 1] = np.concatenate([-np.sin(phase), np.sin(phase)], axis=1)
    return table.astype(np.float32)


def wave_numbers(circle):
    k = np.tile(np.arange(KMAX), 2)
    table = np.zeros((8, LANES))
    table[0] = 4.0 * np.sin(math.pi * k / circle) ** 2
    table[1] = np.where(k == 0, 1.0, 2.0) / circle
    return table.astype(np.float32)


def log_decay(reach, circle):
    u = 0.5 / (reach * circle)
    root = jnp.sqrt(1.0 + u * u)
    return -2.0 * jnp.log1p(u + u * u / (1.0 + root)), 4.0 * u * root


def lane_index(shape):
    return lax.broadcasted_iota(jnp.int32, shape, len(shape) - 1)


def row_index(shape):
    return lax.broadcasted_iota(jnp.int32, shape, len(shape) - 2)


def flux_rows(tracer, zonal, merid, below, above, north, south):
    rows = tracer.shape[0]
    at = row_index(tracer.shape)
    flux = merid * tracer
    up = jnp.where(at == rows - 1, above, pltpu.roll(flux, rows - 1, 0))
    face = north * (flux + up)
    first = south[0:1] * (below + flux[0:1])
    return zonal * tracer, jnp.where(at == 0, first, pltpu.roll(face, 1, 0)) - face


def edge_kernel(tracer, merid, first, last, tracer_rows, merid_rows, sems):
    fields, _, rows, _ = tracer.shape
    tall = tracer_rows.shape[3]
    copies = []
    for side, at in enumerate((0, rows - tall)):
        copies.append(pltpu.make_async_copy(merid.at[:, pl.ds(at, tall)], merid_rows.at[side], sems.at[side]))
        copies.append(
            pltpu.make_async_copy(tracer.at[:, :, pl.ds(at, tall)], tracer_rows.at[side], sems.at[2 + side])
        )
    for copy in copies:
        copy.start()
    for side, (out, at) in enumerate(((first, 0), (last, tall - 1))):
        copies[2 * side].wait()
        copies[2 * side + 1].wait()
        for f in range(fields):
            out[f] = merid_rows[side, :, at] * tracer_rows[side, f, :, at]


def fetch_kernel(bases, info, *refs):
    sems, tables = refs[-1], (len(refs) - 4 - 3 * len(bases)) // 2
    sources, targets = refs[: 3 + tables], refs[3 + tables : -1]
    views = []
    for base in bases:
        level = pl.ds(info[base], targets[1].shape[0])
        views += [sources[0].at[:, level], sources[1].at[level], sources[2].at[level]]
    views += sources[3:]
    copies = [pltpu.make_async_copy(view, target, sems.at[i]) for i, (view, target) in enumerate(zip(views, targets))]
    for copy in copies:
        copy.start()
    for copy in copies:
        copy.wait()


def project_kernel(circle, base, first, last, info, reach, tracer, zonal, merid, below, above, metric, turn, forward, *refs):
    prior = None if first else refs[0]
    coeffs, sums, stack, total_sums = refs[-4:]
    fields, size, rows, cells = tracer.shape
    levels, signals = below.shape[1], fields * rows
    first_level = info[base]
    rows_at = pl.ds(info[2], rows)

    def fluxes(i, f):
        north, south = metric[rows_at, 1:2], metric[rows_at, 2:3]
        at = pl.ds(first_level + i, 1)
        return flux_rows(tracer[f, i], zonal[i], merid[i], below[f, at], above[f, at], north, south)

    @pl.when(info[0] == 1)
    def _():
        table = forward[...]
        turn_cos, turn_sin = turn[info[1], 0:1], turn[info[1], 1:2]
        for group in range(size // PER_STEP):
            slot = 2 * (group % 2)
            for i in range(PER_STEP):
                for f in range(fields):
                    at = pl.ds((i * fields + f) * rows, rows)
                    z, m = fluxes(group * PER_STEP + i, f)
                    stack[slot, at, :cells], stack[slot + 1, at, :cells] = halves(z)
                    stack[slot, at, cells:], stack[slot + 1, at, cells:] = halves(m)
            high = jnp.dot(stack[slot], table, preferred_element_type=f32)
            low = jnp.dot(stack[slot + 1], table, preferred_element_type=f32)
            total = high[:, :LANES] + (high[:, LANES:] + low[:, :LANES] + low[:, LANES:])
            total = total * turn_cos + pltpu.roll(total, KMAX, 1) * turn_sin
            coeffs[group * PER_STEP : (group + 1) * PER_STEP] = total.reshape(PER_STEP, signals, LANES)

    @pl.when(info[0] == 0)
    def _():
        total_sums[...] = jnp.zeros_like(total_sums) if first else prior[...]
        cell = lane_index((1, cells)).astype(f32)
        lane = lane_index((rows, LANES))

        def one(i, _):
            level = first_level + i
            slope, gain = log_decay(jnp.full((1, cells), reach[level], f32), circle)
            eastward = jnp.exp((cells - 1.0 - cell) * slope)
            westward = jnp.exp(cell * slope)
            for f in range(fields):
                at = pl.ds(f * rows, rows)
                z, m = fluxes(i, f)
                z = z * gain
                right = jnp.sum((m + z) * eastward, axis=1, keepdims=True)
                left = jnp.sum((m - z) * westward, axis=1, keepdims=True)
                total_sums[at, :] += jnp.where(lane == level, right, jnp.where(lane == level + levels, left, 0.0))
            return 0

        lax.fori_loop(0, size, one, 0)
        sums[...] = jnp.transpose(total_sums[...])[: 2 * levels] if last else total_sums[...]


def enter_kernel(circle, levels, parts, info, reach, sums, enter):
    @pl.when(info[0] == 0)
    def _():
        cells = circle // parts
        wide = sums.shape[2] // LANES
        listed = row_index((2 * levels, LANES))
        spread = jnp.ones((2 * levels, LANES), f32)
        for level in range(levels):
            spread = jnp.where(listed % levels == level, reach[level], spread)
        slopes, _ = log_decay(spread, circle)
        wrap = 1.0 / (1.0 - jnp.exp(circle * slopes))
        here = info[1]
        total = jnp.zeros(sums.shape[1:], f32)
        for p in range(parts):
            peer = here ^ p
            steps_up = lax.rem(here - peer - 1 + 2 * parts, parts).astype(f32)
            steps_down = lax.rem(peer - here - 1 + 2 * parts, parts).astype(f32)
            steps = jnp.where(listed < levels, steps_up, steps_down)
            weight = jnp.exp(steps * (cells * slopes)) * wrap
            total += sums[p] * jnp.concatenate([weight] * wide, axis=1)
        pad = jnp.zeros((LANES - 2 * levels, wide * LANES), f32)
        enter[...] = jnp.transpose(jnp.concatenate([total, pad], axis=0))


def finish_kernel(circle, parts, base, info, reach, tracer, zonal, merid, below, above, metric, turn, backward, waves, rows_listed, kept, coeffs, enter, *refs):
    out, stack, ready, sems = refs[-4:]
    fields, size, rows, cells = tracer.shape
    levels, signals = below.shape[1], fields * rows
    first_level = info[base]
    rows_at = pl.ds(info[2], rows)

    def send(i, count):
        return pltpu.make_async_copy(
            ready.at[:, pl.ds(i, count)], out.at[:, pl.ds(first_level + i, count)], sems.at[i]
        )

    @pl.when(info[0] == 1)
    def _():
        scale = metric[rows_at, 0:1]
        turn_cos, turn_sin = turn[info[1], 0:1], turn[info[1], 1:2]
        row = info[2] + row_index((rows, 1))
        matches = row == rows_listed[...]
        retained = jnp.sum(jnp.where(matches, kept[...], 0), axis=1, keepdims=True)
        number = lane_index((rows, LANES)) % KMAX
        keep = jnp.where(number < retained, waves[1:2] * scale, 0.0)
        for group in range(size // PER_STEP):
            slot = group % 2
            for i in range(PER_STEP):
                level = first_level + group * PER_STEP + i
                coupling = (jnp.full((1, LANES), reach[level], f32) * circle) ** 2
                weight = keep / (1.0 + coupling * waves[0:1])
                for f in range(fields):
                    at = pl.ds((i * fields + f) * rows, rows)
                    c = coeffs[group * PER_STEP + i, f * rows : (f + 1) * rows] * weight
                    c = c * turn_cos - pltpu.roll(c, KMAX, 1) * turn_sin
                    hi, lo = halves(c)
                    stack[slot, at, :LANES], stack[slot, at, LANES : 2 * LANES] = hi, lo
                    stack[slot, at, 2 * LANES : 3 * LANES], stack[slot, at, 3 * LANES :] = hi, lo
            change = jnp.dot(stack[slot, : PER_STEP * signals], backward[...], preferred_element_type=f32)
            for i in range(PER_STEP):
                for f in range(fields):
                    at = (i * fields + f) * rows
                    level = group * PER_STEP + i
                    ready[f, level] = tracer[f, level] + change[at : at + rows]
            send(group * PER_STEP, PER_STEP).start()
        for group in range(size // PER_STEP):
            send(group * PER_STEP, PER_STEP).wait()

    @pl.when(info[0] == 0)
    def _():
        scale, north, south = metric[rows_at, 0:1], metric[rows_at, 1:2], metric[rows_at, 2:3]
        blocks = cells // LANES
        near = lane_index((LANES, LANES)) - row_index((LANES, LANES))
        lane = lane_index((1, LANES)).astype(f32)
        pick = lane_index((rows, LANES))

        def one(i, _):
            level = first_level + i
            level_at = pl.ds(level, 1)
            slope, gain = log_decay(jnp.full((1, LANES), reach[level], f32), circle)
            root = 1.0 / jnp.sqrt(1.0 + 4.0 * (jnp.full((1, LANES), reach[level], f32) * circle) ** 2)
            decay = jnp.exp(jnp.abs(near).astype(f32) * slope)
            turned = jnp.where(near > 0, gain, jnp.where(near < 0, -gain, 0.0)) * decay
            zhi, zlo = halves(turned)
            mhi, mlo = halves(decay)
            table = jnp.concatenate([jnp.concatenate([zhi, zlo], axis=1), jnp.concatenate([mhi, mlo], axis=1)], axis=0)
            for f in range(fields):
                z, m = flux_rows(
                    tracer[f, i], zonal[i], merid[i], below[f, level_at], above[f, level_at], north, south
                )
                for b in range(blocks):
                    at = slice((b * fields + f) * rows, (b * fields + f + 1) * rows)
                    own = slice(b * LANES, (b + 1) * LANES)
                    hi, lo = halves(z[:, own])
                    stack[0, at, :LANES], stack[0, at, 2 * LANES : 3 * LANES] = hi, lo
                    hi, lo = halves(m[:, own])
                    stack[0, at, LANES : 2 * LANES], stack[0, at, 3 * LANES :] = hi, lo
            used = blocks * signals
            high = jnp.dot(stack[0, :used, : 2 * LANES], table, preferred_element_type=f32)
            low = jnp.dot(stack[0, :used, 2 * LANES :], table, preferred_element_type=f32)
            local = high[:, :LANES] + (high[:, LANES:] + low[:, :LANES] + low[:, LANES:])
            from_west = jnp.exp((lane + 1.0) * slope)
            from_east = jnp.exp((LANES - lane) * slope)
            across = jnp.exp(LANES * slope)[:, 0:1]
            size_of = root * scale
            edge = gain[:, 0:1]
            for f in range(fields):
                entering = enter[f * rows : (f + 1) * rows]
                part = [local[(b * fields + f) * rows : (b * fields + f + 1) * rows] for b in range(blocks)]
                carry = jnp.sum(jnp.where(pick == level, entering, 0.0), axis=1, keepdims=True)
                ups = []
                for b in range(blocks):
                    ups.append(carry)
                    cell = slice((b + 1) * LANES - 1, (b + 1) * LANES)
                    flux = zonal[i, :, cell] * tracer[f, i, :, cell]
                    carry = across * carry + (part[b][:, LANES - 1 :] + edge * flux)
                carry = jnp.sum(jnp.where(pick == level + levels, entering, 0.0), axis=1, keepdims=True)
                for b in reversed(range(blocks)):
                    own = slice(b * LANES, (b + 1) * LANES)
                    change = part[b] + from_west * ups[b] + from_east * carry
                    ready[f, i, :, own] = tracer[f, i, :, own] + size_of * change
                    cell = slice(b * LANES, b * LANES + 1)
                    flux = zonal[i, :, cell] * tracer[f, i, :, cell]
                    carry = across * carry + (part[b][:, :1] - edge * flux)
            send(i, 1).start()
            return 0

        lax.fori_loop(0, size, one, 0)
        for i in range(size):
            send(i, 1).wait()


def swapped(array, bit, lats, parts):
    pairs = [(lat * parts + p, lat * parts + (p ^ bit)) for lat in lats for p in range(parts)]
    return lax.ppermute(array, AXES, pairs)


def on_device(tracer, zonal, merid, filt_rows, keep_modes, reach):
    fields, levels, rows, cells = tracer.shape
    bands, parts = lax.axis_size("lat"), lax.axis_size("lon")
    circle, signals = cells * parts, fields * rows
    padded = -(-signals // LANES) * LANES
    listed = filt_rows.shape[0]
    assert listed == 2 * rows and 2 * levels <= LANES and cells % LANES == 0
    assert parts >= 2 and parts & (parts - 1) == 0 and bands > 2 and rows % 8 == 0
    band, place = lax.axis_index("lat"), lax.axis_index("lon")
    polar = jnp.logical_or(band == 0, band == bands - 1).astype(jnp.int32)
    bit = (place & 1) * polar
    half, chunk = levels // 2, levels // 2 // CHUNKS
    assert levels % (2 * CHUNKS * PER_STEP) == 0
    starts = [side * half + c * chunk for side in (1 - bit, bit) for c in range(CHUNKS)]
    info = jnp.stack([polar, place, band * rows] + starts).astype(jnp.int32)
    sent_at, own_at = range(3, 3 + CHUNKS), range(3 + CHUNKS, 3 + 2 * CHUNKS)
    poles, inner = (0, bands - 1), range(1, bands - 1)

    smem, vmem, hbm = (pl.BlockSpec(memory_space=space) for space in (pltpu.SMEM, pltpu.VMEM, pltpu.HBM))
    params = pltpu.CompilerParams(vmem_limit_bytes=VMEM_LIMIT)
    dma = pltpu.SemaphoreType.DMA

    tall = 8
    resident = lambda array: pltpu.with_memory_space_constraint(array, pltpu.HBM)
    first, last = pl.pallas_call(
        edge_kernel,
        out_shape=(jax.ShapeDtypeStruct((fields, levels, cells), f32),) * 2,
        in_specs=[hbm, hbm],
        out_specs=(vmem, vmem),
        scratch_shapes=[
            pltpu.VMEM((2, fields, levels, tall, cells), f32),
            pltpu.VMEM((2, levels, tall, cells), f32),
            dma((4,)),
        ],
        compiler_params=params,
        name="edges",
    )(resident(tracer), resident(merid))
    below = lax.ppermute(last, "lat", [(i, i + 1) for i in range(bands - 1)])
    above = lax.ppermute(first, "lat", [(i + 1, i) for i in range(bands - 1)])
    forward, waves_at = wave_tables(cells, circle)
    forward = jnp.asarray(np.concatenate(split_table(forward), axis=1))
    hi, lo = split_table(waves_at)
    backward = jnp.asarray(np.concatenate([hi, hi, lo, lo], axis=0))
    metric = jnp.asarray(metric_table(rows * bands))
    turn = jnp.asarray(turn_table(parts, cells, circle))
    waves = jnp.asarray(wave_numbers(circle))
    tables = (forward, backward, metric, turn, waves)
    bases = (*sent_at, *own_at)
    whole, course = (fields, levels, rows, cells), (chunk, rows, cells)
    shapes = [(fields, *course), course, course] * len(bases)
    types = [pltpu.VMEM(shape, f32) for shape in shapes] + [pltpu.VMEM(t.shape, t.dtype) for t in tables]
    fetched = pl.pallas_call(
        functools.partial(fetch_kernel, bases),
        out_shape=types,
        in_specs=[smem] + [hbm] * (3 + len(tables)),
        out_specs=[vmem] * len(types),
        scratch_shapes=[dma((len(types),))],
        compiler_params=params,
        cost_estimate=pl.CostEstimate(flops=0, transcendentals=0, bytes_accessed=16 << 20),
        name="fetch",
    )(info, *map(resident, (tracer, zonal, merid, *tables)))
    held = {base: fetched[3 * i : 3 * i + 3] for i, base in enumerate(bases)}
    forward, backward, metric, turn, waves = fetched[3 * len(bases) :]

    def project(base, last, *prior):
        return pl.pallas_call(
            functools.partial(project_kernel, circle, base, not prior, last),
            out_shape=(
                jax.ShapeDtypeStruct((chunk, signals, LANES), f32),
                jax.ShapeDtypeStruct((2 * levels, padded) if last else (padded, LANES), f32),
            ),
            in_specs=[smem] * 2 + [vmem] * (8 + len(prior)),
            out_specs=(vmem, vmem),
            scratch_shapes=[
                pltpu.VMEM((4, PER_STEP * signals, 2 * cells), bf16),
                pltpu.VMEM((padded, LANES), f32),
            ],
            compiler_params=params,
            name="project",
        )(info, reach, *held[base], below, above, metric, turn, forward, *prior)

    def finish(base, coeffs, *prior):
        return pl.pallas_call(
            functools.partial(finish_kernel, circle, parts, base),
            out_shape=jax.ShapeDtypeStruct(whole, f32),
            in_specs=[smem] * 2 + [vmem] * 13 + [hbm] * len(prior),
            out_specs=hbm,
            scratch_shapes=[
                pltpu.VMEM((2, max(cells // LANES, PER_STEP) * signals, 4 * LANES), bf16),
                pltpu.VMEM((fields, chunk, rows, cells), f32),
                dma((chunk,)),
            ],
            input_output_aliases={15: 0} if prior else {},
            compiler_params=params,
            name="finish",
        )(
            info, reach, *held[base], below, above, metric, turn, backward, waves,
            filt_rows.reshape(1, listed), keep_modes.reshape(1, listed), coeffs, enter, *prior,
        )

    def summed(total):
        step, stacked = 2, []
        while 2 * step < parts:
            size = total.shape[0] // 2
            side = (place // step) & 1
            mine = lax.dynamic_slice_in_dim(total, side * size, size, 0)
            other = lax.dynamic_slice_in_dim(total, (1 - side) * size, size, 0)
            total = mine + swapped(other, step, poles, parts)
            stacked.append(step)
            step *= 2
        if step < parts:
            total = total + swapped(total, step, poles, parts)
        for step in reversed(stacked):
            back = swapped(total, step, poles, parts)
            side = ((place // step) & 1) == 0
            total = jnp.concatenate([jnp.where(side, total, back), jnp.where(side, back, total)], axis=0)
        return total

    sums, totals = (), []
    for c in range(CHUNKS):
        sent, *sums = project(sent_at[c], False, *sums)
        received = swapped(sent, 1, poles, parts)
        own, *sums = project(own_at[c], c == CHUNKS - 1, *sums)
        totals.append(summed(own + received))

    gathered = sums[0][None]
    step = 1
    while step < parts:
        gathered = jnp.concatenate([gathered, swapped(gathered, step, inner, parts)], axis=0)
        step *= 2
    enter = pl.pallas_call(
        functools.partial(enter_kernel, circle, levels, parts),
        out_shape=jax.ShapeDtypeStruct((padded, LANES), f32),
        in_specs=[smem, smem, vmem],
        out_specs=vmem,
        compiler_params=params,
        name="enter",
    )(info, reach, gathered)

    rest = [swapped(total, 1, poles, parts) for total in totals]
    result = ()
    for base, coeffs in zip([*own_at, *sent_at], totals + rest):
        result = (finish(base, coeffs, *result),)
    return result[0]


def solution(mesh):
    return jax.shard_map(
        on_device,
        mesh=mesh,
        in_specs=(
            P(None, None, "lat", "lon"),
            P(None, "lat", "lon"),
            P(None, "lat", "lon"),
            P(),
            P(),
            P(),
        ),
        out_specs=P(None, None, "lat", "lon"),
        check_vma=False,
    )
```
